32 devices in a mesh: row: 8 (over z, y), col: 4 (over x, core).
Axes of the slice: x: 2, y: 2, z: 4, core: 2. Of those that a mesh axis runs over, the one named last changes fastest.
Arguments:
- obs_panel: bfloat16 [196608, 2048], P('row', 'col'), may hold values from -0.1875 to 0.1875
- skies: bfloat16 [196608, 256], P('row', 'col'), may hold values from -6 to 6
- panel_index: int32 [2048], replicated, may hold values from 0 to 196607
- prior_sum: float32 [196608, 256], P('row', 'col'), may hold values from -6 to 6
- apod: float32 [196608], P('row'), may hold values from 0.05 to 1
- proj_panel: bfloat16 [2048, 196608], P(None, ('row', 'col')), may hold values from -0.02734375 to 0.02734375
Outputs:
- reobserved: float32 [196608, 256], P('row', 'col')
- projection: float32 [2048, 256], P('row', 'col')
The draws below stay inside these ranges and needn't reach their ends.
Inputs may be any that keep to these rules, and one draw needn't show every extreme that they name: `panel_index`: rows of the observed patch; a row may appear more than once.
All inputs are finite; a program needn't handle non-finite values.
Results may differ from the reference program's by a relative error of at most 0.0029.
Values may be sent and summed in bfloat16 or wider, within the bound.
A program may use at most 192 MiB of HBM per device.

```python
import math
import jax
import jax.numpy as jnp

NP = 196608
PANEL = 2048
NSIM = 256
PROWS = 2048


def set_ends(array, own_key, least, top_value):
    spot = [jax.random.randint(jax.random.fold_in(own_key, axis), (), 0, length) for axis, length in enumerate(array.shape)]
    longest = array.shape.index(max(array.shape))
    next_to = spot[:longest] + [(spot[longest] + 1) % array.shape[longest]] + spot[longest + 1:]
    return array.at[tuple(spot)].set(least).at[tuple(next_to)].set(top_value)


def with_spikes(entries, own_key, source, target, parts, factor):
    owner, partner = [(jnp.arange(entries.shape[dim]) // (entries.shape[dim] // parts)).reshape([-1 if axis == dim else 1 for axis in range(entries.ndim)]) for dim in (source, target)]
    chosen = jax.random.permutation(own_key, parts)[partner]
    strong = (owner == chosen) | (owner == (partner + parts // 2) % parts)
    return jnp.where(strong, factor * entries, entries)


def block_scale(key, dims, shards, low, largest):
    loudness, own = 1.0, jax.random.fold_in(key, 6)
    for axis_at, blocks in shards:
        steps = jnp.exp(jax.random.uniform(jax.random.fold_in(own, axis_at), (blocks,), jnp.float32, low / len(shards), largest / len(shards)))
        loudness = loudness * jnp.repeat(steps, dims[axis_at] // blocks).reshape([-1 if axis == axis_at else 1 for axis in range(len(dims))])
    return loudness


def bell_draw(own_key, dims, deviation, bound, split=(), dtype=jnp.bfloat16):
    result = jax.random.normal(own_key, dims, jnp.float32) * deviation
    if len(split) > 0:
        result = block_scale(own_key, dims, split, -0.22, 0.18) * result
    return jnp.clip(result, min=-bound, max=bound).astype(dtype)


def gaussian_with(own_key, extent, width, most, pieces, heavy, held_as=jnp.bfloat16):
    values = width * jax.random.normal(own_key, extent, jnp.float32)
    if pieces:
        values = values * block_scale(own_key, extent, pieces, -0.22, 0.18)
    return jnp.clip(with_spikes(values, jax.random.fold_in(own_key, 3), *heavy), -most, most).astype(held_as)


def setup_inputs(seed: int = 0) -> dict:
    arg_keys = jax.random.split(jax.random.key(seed), 7)
    return {
        "obs_panel": gaussian_with(arg_keys[0], (NP, PANEL), PANEL ** -0.5, 0.1875, ((0, 8), (1, 4)), (1, 0, 8, 2.0)),
        "skies": bell_draw(arg_keys[1], (NP, NSIM), 1.0, 6.0, ((0, 8), (1, 4))),
        "panel_index": set_ends(jax.random.randint(arg_keys[2], (PANEL,), 0, NP), jax.random.fold_in(arg_keys[2], 1), 0, NP - 1).astype(jnp.int32),
        "prior_sum": bell_draw(arg_keys[3], (NP, NSIM), 1.0, 6.0, ((0, 8), (1, 4)), jnp.float32),
        "apod": jnp.clip(jnp.exp(math.log(1.0) - 2.9957323 * jax.random.uniform(arg_keys[4], (NP,), jnp.float32) ** block_scale(arg_keys[4], (NP,), ((0, 8),), -0.2, 0.2)), 0.05, 1.0),
        "proj_panel": gaussian_with(arg_keys[5], (PROWS, NP), NP ** -0.5, 0.02734375, ((1, 32),), (1, 0, 32, 2.75)),
    }


def reference(obs_panel, skies, panel_index, prior_sum, apod, proj_panel):
    picked = jnp.take(skies, panel_index, axis=0)
    reobserved = prior_sum + jnp.dot(obs_panel, picked, preferred_element_type=jnp.float32)
    weighted = (apod[:, None] * reobserved).astype(jnp.bfloat16)
    projection = jnp.dot(proj_panel, weighted, preferred_element_type=jnp.float32)
    return reobserved, projection
```

```python
import functools
import math

import jax
import jax.numpy as jnp
from jax import lax
from jax.experimental import pallas as pl
from jax.experimental.pallas import tpu as pltpu
from jax.sharding import PartitionSpec as P

MESH = pl.DeviceIdType.MESH
NT = (((1,), (1,)), ((), ()))
CHUNKS = 6
LIMIT = 48 * 1024 * 1024


def remote(src, dst, send, recv, row, col):
    return pltpu.make_async_remote_copy(
        src_ref=src, dst_ref=dst, send_sem=send, recv_sem=recv, device_id=(row, col), device_id_type=MESH
    )


def spread_kernel(n_row, n_col, own_ref, out_ref, land, mine, gather, send1, recv1, send2, recv2):
    r, c = lax.axis_index("row"), lax.axis_index("col")
    sims, panel = own_ref.shape
    part = panel // n_row
    rep = n_row // n_col
    first = []
    for d in range(1, n_row):
        to = lax.rem(r + d, n_row)
        cp = remote(own_ref.at[:, pl.ds(pl.multiple_of(to * part, part), part)], land.at[d - 1],
                    send1.at[d - 1], recv1.at[d - 1], to, c)
        cp.start()
        first.append(cp)
    total = own_ref[:, pl.ds(pl.multiple_of(r * part, part), part)].astype(jnp.float32)
    for d in range(1, n_row):
        first[d - 1].wait_recv()
        total = total + land[d - 1].astype(jnp.float32)
    mine[...] = total.astype(mine.dtype)
    sub = lax.rem(r, rep)
    col_to = lax.div(r, rep)
    slot = sub * n_col + c
    second = []
    for d in range(n_row):
        to = lax.rem(r + d, n_row)
        cp = remote(mine, gather.at[slot], send2.at[d], recv2.at[slot], to, col_to)
        second.append(cp)
        if d > 0:
            cp.start()
        else:
            @pl.when(col_to != c)
            def _():
                cp.start()

            @pl.when(col_to == c)
            def _():
                gather[slot] = mine[...]
    for s in range(rep):
        for j in range(n_col):
            here = (c * rep + s == r) & (c == j)

            @pl.when(jnp.logical_not(here))
            def _():
                remote(mine, gather.at[s * n_col + j], send2.at[0], recv2.at[s * n_col + j], r, c).wait_recv()
    chips = n_col // 2
    core, chip = lax.rem(c, 2), lax.div(c, 2)
    for q in range(n_col):
        other, shift = q // chips, q % chips
        source = lax.rem(chip + shift, chips) * 2 + (core if other == 0 else 1 - core)
        for s in range(rep):
            out_ref[q * sims:(q + 1) * sims, s * part:(s + 1) * part] = gather[s * n_col + source]
    for cp in first:
        cp.wait_send()
    for d in range(n_row):
        if d > 0:
            second[d].wait_send()
        else:
            @pl.when(col_to != c)
            def _():
                second[0].wait_send()


def spread(own, n_row, n_col):
    sims, panel = own.shape
    part = panel // n_row
    vmem = pl.BlockSpec(memory_space=pltpu.VMEM)
    return pl.pallas_call(
        functools.partial(spread_kernel, n_row, n_col),
        out_shape=jax.ShapeDtypeStruct((sims * n_col, panel // n_col), own.dtype),
        in_specs=[vmem],
        out_specs=vmem,
        scratch_shapes=[
            pltpu.VMEM((n_row - 1, sims, part), own.dtype),
            pltpu.VMEM((sims, part), own.dtype),
            pltpu.VMEM((n_row, sims, part), own.dtype),
            pltpu.SemaphoreType.DMA((n_row - 1,)),
            pltpu.SemaphoreType.DMA((n_row - 1,)),
            pltpu.SemaphoreType.DMA((n_row,)),
            pltpu.SemaphoreType.DMA((n_row,)),
        ],
        compiler_params=pltpu.CompilerParams(has_side_effects=True, vmem_limit_bytes=LIMIT),
        name="spread",
    )(own)


def fold_kernel(n_row, n_col, acc_ref, out_ref, land_a, sum_a, land_b, sum_b, land_c, sa, ra, sb, rb, sc, rc):
    r, c = lax.axis_index("row"), lax.axis_index("col")
    chips = n_col // 2
    core, chip = lax.rem(c, 2), lax.div(c, 2)
    out_rows = out_ref.shape[1]

    def block(col):
        return lax.rem(c - col + n_col, n_col)

    a = []
    for b in range(chips):
        to = lax.rem(chip + b, chips)
        cp = remote(acc_ref.at[block(to * 2 + 1 - core)], land_a.at[b], sa.at[b], ra.at[b], r, chip * 2 + 1 - core)
        cp.start()
        a.append(cp)
    bs = []
    for s in list(range(1, chips)) + [0]:
        to = lax.rem(chip + s, chips)
        a[s].wait_recv()
        sum_a[s] = acc_ref[block(to * 2 + core)] + land_a[s]
        if s > 0:
            cp = remote(sum_a.at[s], land_b.at[s - 1], sb.at[s - 1], rb.at[s - 1], r, to * 2 + core)
            cp.start()
            bs.append(cp)
    total = sum_a[0]
    for s in range(1, chips):
        bs[s - 1].wait_recv()
        total = total + land_b[s - 1]
    sum_b[...] = total
    cs = []
    for d in range(1, n_row):
        to = lax.rem(r + d, n_row)
        cp = remote(sum_b.at[:, pl.ds(pl.multiple_of(to * out_rows, out_rows), out_rows)], land_c.at[d - 1],
                    sc.at[d - 1], rc.at[d - 1], to, c)
        cp.start()
        cs.append(cp)
    total = sum_b[:, pl.ds(pl.multiple_of(r * out_rows, out_rows), out_rows)]
    for d in range(1, n_row):
        cs[d - 1].wait_recv()
        total = total + land_c[d - 1]
    out_ref[...] = total
    for cp in a + bs + cs:
        cp.wait_send()


def fold(acc, n_row, n_col):
    _, sims, prows = acc.shape
    chips = n_col // 2
    vmem = pl.BlockSpec(memory_space=pltpu.VMEM)
    dma = pltpu.SemaphoreType.DMA
    return pl.pallas_call(
        functools.partial(fold_kernel, n_row, n_col),
        out_shape=jax.ShapeDtypeStruct((sims, prows // n_row), jnp.float32),
        in_specs=[vmem],
        out_specs=vmem,
        scratch_shapes=[
            pltpu.VMEM((chips, sims, prows), jnp.float32),
            pltpu.VMEM((chips, sims, prows), jnp.float32),
            pltpu.VMEM((chips - 1, sims, prows), jnp.float32),
            pltpu.VMEM((sims, prows), jnp.float32),
            pltpu.VMEM((n_row - 1, sims, prows // n_row), jnp.float32),
            dma((chips,)), dma((chips,)), dma((chips - 1,)), dma((chips - 1,)), dma((n_row - 1,)), dma((n_row - 1,)),
        ],
        compiler_params=pltpu.CompilerParams(has_side_effects=True, vmem_limit_bytes=LIMIT),
        name="fold",
    )(acc)


def panel_dot(picked, obs, t, chunks, n_col, sims):
    depth = obs.shape[1]
    size = obs.shape[0] // n_col // chunks
    kept = picked.shape[0] // 2

    def body(p_ref, o_ref, keep_ref, send_ref):
        value = lax.dot_general(p_ref[...], o_ref[...], NT, preferred_element_type=jnp.float32)
        keep_ref[...] = value[:kept]
        send_ref[...] = value[kept:].astype(jnp.bfloat16)

    return pl.pallas_call(
        body,
        grid=(n_col,),
        in_specs=[pl.BlockSpec(picked.shape, lambda i: (0, 0)), pl.BlockSpec((size, depth), lambda i: (i * chunks + t, 0))],
        out_specs=[pl.BlockSpec((kept, size), lambda i: (0, i))] * 2,
        out_shape=[jax.ShapeDtypeStruct((kept, n_col * size), d) for d in (jnp.float32, jnp.bfloat16)],
        cost_estimate=pl.CostEstimate(flops=2 * picked.size * n_col * size, bytes_accessed=n_col * size * (2 * depth + 6 * kept), transcendentals=0),
        compiler_params=pltpu.CompilerParams(vmem_limit_bytes=LIMIT),
        name="panel_dot",
    )(picked, obs)


def combine(col, keep, near, far, prior, apod, out, t, chunks, n_col):
    sims = prior.shape[0]
    size = prior.shape[1] // n_col // chunks
    n_far = len(far)

    def body(c_ref, keep_ref, near_ref, *refs):
        fars, prior_ref, apod_ref = refs[:n_far], refs[n_far], refs[n_far + 1]
        re_ref, w_ref = refs[-2], refs[-1]
        total = keep_ref[...] + near_ref[...].astype(jnp.float32)
        for f in fars:
            total = total + f[...].astype(jnp.float32)
        total = prior_ref[...] + total
        re_ref[...] = total
        w_ref[0] = (apod_ref[...] * total).astype(jnp.bfloat16)

    def slab(i, c):
        return lax.rem(c[0] + i, n_col)

    part = pl.BlockSpec((sims, size), lambda i, c: (0, slab(i, c)))
    whole = pl.BlockSpec((sims, size), lambda i, c: (0, slab(i, c) * chunks + t))
    line = pl.BlockSpec((1, size), lambda i, c: (0, slab(i, c) * chunks + t))
    specs = [part] * (2 + n_far) + [whole, line]
    args = [keep, near, *far, prior, apod]
    alias = {}
    if out is not None:
        specs.append(pl.BlockSpec(memory_space=pl.ANY))
        args.append(out)
        alias = {len(args): 0}
    return pl.pallas_call(
        body,
        grid_spec=pltpu.PrefetchScalarGridSpec(
            num_scalar_prefetch=1,
            grid=(n_col,),
            in_specs=specs,
            out_specs=[whole, pl.BlockSpec((1, sims, size), lambda i, c: (i, 0, 0))],
        ),
        out_shape=[jax.ShapeDtypeStruct(prior.shape, jnp.float32), jax.ShapeDtypeStruct((n_col, sims, size), jnp.bfloat16)],
        input_output_aliases=alias,
        cost_estimate=pl.CostEstimate(flops=4 * sims * size * n_col, bytes_accessed=sims * size * n_col * 20, transcendentals=0),
        compiler_params=pltpu.CompilerParams(vmem_limit_bytes=LIMIT),
        name="combine",
    )(col, *args)


def project(parts, proj, acc, t, chunks):
    n, (sims, size) = len(parts), parts[0].shape
    prows = proj.shape[0]
    tile = min(512, prows)

    def body(*refs):
        w = jnp.concatenate([refs[i][...] for i in range(n)], axis=0)
        value = lax.dot_general(w, refs[n][...], NT, preferred_element_type=jnp.float32)
        for i in range(n):
            block = value[i * sims:(i + 1) * sims]
            refs[-1][i] = block if acc is None else refs[n + 1][i] + block

    block = pl.BlockSpec((n, sims, tile), lambda q: (0, 0, q))
    specs = [pl.BlockSpec((sims, size), lambda q: (0, 0))] * n + [pl.BlockSpec((tile, size), lambda q: (q, t))]
    args = [*parts, proj]
    alias = {}
    if acc is not None:
        specs.append(block)
        alias = {len(args): 0}
        args.append(acc)
    return pl.pallas_call(
        body,
        grid=(prows // tile,),
        in_specs=specs,
        out_specs=block,
        out_shape=jax.ShapeDtypeStruct((n, sims, prows), jnp.float32),
        input_output_aliases=alias,
        cost_estimate=pl.CostEstimate(flops=2 * n * sims * size * prows, bytes_accessed=2 * size * prows + 8 * n * sims * prows, transcendentals=0),
        compiler_params=pltpu.CompilerParams(vmem_limit_bytes=LIMIT),
        name="project",
    )(*args)


def on_device(n_row, n_col, obs_panel, skies, panel_index, prior_sum, apod, proj_panel):
    rows_blk, sims = skies.shape
    c = lax.axis_index("col")
    local_idx = panel_index - lax.axis_index("row") * rows_blk
    inside = (local_idx >= 0) & (local_idx < rows_blk)
    taken = jnp.take(skies, jnp.clip(local_idx, 0, rows_blk - 1), axis=0)
    own = jnp.where(inside[:, None], taken, jnp.zeros((), jnp.bfloat16)).T
    picked = spread(own, n_row, n_col)

    chunks = math.gcd(CHUNKS, rows_blk // n_col // 128)
    chips = n_col // 2
    swap = [(i, i ^ 1) for i in range(n_col)]
    prior, line = prior_sum.T, apod[None, :]
    col = c.astype(jnp.int32)[None]
    out, acc = None, None
    for t in range(chunks):
        keep, send = panel_dot(picked, obs_panel, t, chunks, n_col, sims)
        near = lax.ppermute(send, "col", swap)
        far = []
        for s in range(1, chips):
            away = slice(s * sims, (s + 1) * sims)
            value = (keep[away] + near[away].astype(jnp.float32)).astype(jnp.bfloat16)
            far.append(lax.ppermute(value, "col", [(i, (i + 2 * s) % n_col) for i in range(n_col)]))
        out, weighted = combine(col, keep, near, far, prior, line, out, t, chunks, n_col)
        parts = [weighted[0]]
        for d in range(1, n_col):
            parts.append(lax.ppermute(weighted[d], "col", [(i, (i + d) % n_col) for i in range(n_col)]))
        acc = project(parts, proj_panel, acc, t, chunks)
    projection = fold(acc, n_row, n_col)
    return out.T, projection.T


def solution(mesh):
    in_specs = (P("row", "col"), P("row", "col"), P(), P("row", "col"), P("row"), P(None, ("row", "col")))
    out_specs = (P("row", "col"), P("row", "col"))
    body = functools.partial(on_device, mesh.shape["row"], mesh.shape["col"])
    return jax.shard_map(body, mesh=mesh, in_specs=in_specs, out_specs=out_specs, check_vma=False)
```

```python
import functools
import math

import jax
import jax.numpy as jnp
from jax import lax
from jax.experimental import pallas as pl
from jax.experimental.pallas import tpu as pltpu
from jax.sharding import PartitionSpec as P

MESH = pl.DeviceIdType.MESH
NT = (((1,), (1,)), ((), ()))
UNIT = 256
D2, D3, D4 = 1, 3, 5
LIMIT = 48 * 1024 * 1024


def remote(src, dst, send, recv, row, col):
    return pltpu.make_async_remote_copy(
        src_ref=src, dst_ref=dst, send_sem=send, recv_sem=recv, device_id=(row, col), device_id_type=MESH
    )


def spread_kernel(n_row, n_col, own_ref, out_ref, land, mine, gather, send1, recv1, send2, recv2):
    r, c = lax.axis_index("row"), lax.axis_index("col")
    sims, panel = own_ref.shape
    part = panel // n_row
    rep = n_row // n_col
    first = []
    for d in range(1, n_row):
        to = lax.rem(r + d, n_row)
        cp = remote(own_ref.at[:, pl.ds(pl.multiple_of(to * part, part), part)], land.at[d - 1],
                    send1.at[d - 1], recv1.at[d - 1], to, c)
        cp.start()
        first.append(cp)
    total = own_ref[:, pl.ds(pl.multiple_of(r * part, part), part)].astype(jnp.float32)
    for d in range(1, n_row):
        first[d - 1].wait_recv()
        total = total + land[d - 1].astype(jnp.float32)
    mine[...] = total.astype(mine.dtype)
    sub = lax.rem(r, rep)
    col_to = lax.div(r, rep)
    slot = sub * n_col + c
    second = []
    for d in range(n_row):
        to = lax.rem(r + d, n_row)
        cp = remote(mine, gather.at[slot], send2.at[d], recv2.at[slot], to, col_to)
        second.append(cp)
        if d > 0:
            cp.start()
        else:
            @pl.when(col_to != c)
            def _():
                cp.start()

            @pl.when(col_to == c)
            def _():
                gather[slot] = mine[...]
    for s in range(rep):
        for j in range(n_col):
            here = (c * rep + s == r) & (c == j)

            @pl.when(jnp.logical_not(here))
            def _():
                remote(mine, gather.at[s * n_col + j], send2.at[0], recv2.at[s * n_col + j], r, c).wait_recv()
    chips = n_col // 2
    core, chip = lax.rem(c, 2), lax.div(c, 2)
    for q in range(n_col):
        other, shift = q // chips, q % chips
        source = lax.rem(chip + shift, chips) * 2 + (core if other == 0 else 1 - core)
        for s in range(rep):
            out_ref[q * sims:(q + 1) * sims, s * part:(s + 1) * part] = gather[s * n_col + source]
    for cp in first:
        cp.wait_send()
    for d in range(n_row):
        if d > 0:
            second[d].wait_send()
        else:
            @pl.when(col_to != c)
            def _():
                second[0].wait_send()


def spread(own, n_row, n_col):
    sims, panel = own.shape
    part = panel // n_row
    vmem = pl.BlockSpec(memory_space=pltpu.VMEM)
    return pl.pallas_call(
        functools.partial(spread_kernel, n_row, n_col),
        out_shape=jax.ShapeDtypeStruct((sims * n_col, panel // n_col), own.dtype),
        in_specs=[vmem],
        out_specs=vmem,
        scratch_shapes=[
            pltpu.VMEM((n_row - 1, sims, part), own.dtype),
            pltpu.VMEM((sims, part), own.dtype),
            pltpu.VMEM((n_row, sims, part), own.dtype),
            pltpu.SemaphoreType.DMA((n_row - 1,)),
            pltpu.SemaphoreType.DMA((n_row - 1,)),
            pltpu.SemaphoreType.DMA((n_row,)),
            pltpu.SemaphoreType.DMA((n_row,)),
        ],
        compiler_params=pltpu.CompilerParams(has_side_effects=True, vmem_limit_bytes=LIMIT),
        name="spread",
    )(own)


def fold_kernel(n_row, n_col, acc_ref, out_ref, land_a, sum_a, land_b, sum_b, land_c, sa, ra, sb, rb, sc, rc):
    r, c = lax.axis_index("row"), lax.axis_index("col")
    chips = n_col // 2
    core, chip = lax.rem(c, 2), lax.div(c, 2)
    out_rows = out_ref.shape[1]

    def block(col):
        return lax.rem(c - col + n_col, n_col)

    a = []
    for b in range(chips):
        to = lax.rem(chip + b, chips)
        cp = remote(acc_ref.at[block(to * 2 + 1 - core)], land_a.at[b], sa.at[b], ra.at[b], r, chip * 2 + 1 - core)
        cp.start()
        a.append(cp)
    bs = []
    for s in list(range(1, chips)) + [0]:
        to = lax.rem(chip + s, chips)
        a[s].wait_recv()
        sum_a[s] = acc_ref[block(to * 2 + core)] + land_a[s]
        if s > 0:
            cp = remote(sum_a.at[s], land_b.at[s - 1], sb.at[s - 1], rb.at[s - 1], r, to * 2 + core)
            cp.start()
            bs.append(cp)
    total = sum_a[0]
    for s in range(1, chips):
        bs[s - 1].wait_recv()
        total = total + land_b[s - 1]
    sum_b[...] = total
    cs = []
    for d in range(1, n_row):
        to = lax.rem(r + d, n_row)
        cp = remote(sum_b.at[:, pl.ds(pl.multiple_of(to * out_rows, out_rows), out_rows)], land_c.at[d - 1],
                    sc.at[d - 1], rc.at[d - 1], to, c)
        cp.start()
        cs.append(cp)
    total = sum_b[:, pl.ds(pl.multiple_of(r * out_rows, out_rows), out_rows)]
    for d in range(1, n_row):
        cs[d - 1].wait_recv()
        total = total + land_c[d - 1]
    out_ref[...] = total
    for cp in a + bs + cs:
        cp.wait_send()


def fold(acc, n_row, n_col):
    _, sims, prows = acc.shape
    chips = n_col // 2
    vmem = pl.BlockSpec(memory_space=pltpu.VMEM)
    dma = pltpu.SemaphoreType.DMA
    return pl.pallas_call(
        functools.partial(fold_kernel, n_row, n_col),
        out_shape=jax.ShapeDtypeStruct((sims, prows // n_row), jnp.float32),
        in_specs=[vmem],
        out_specs=vmem,
        scratch_shapes=[
            pltpu.VMEM((chips, sims, prows), jnp.float32),
            pltpu.VMEM((chips, sims, prows), jnp.float32),
            pltpu.VMEM((chips - 1, sims, prows), jnp.float32),
            pltpu.VMEM((sims, prows), jnp.float32),
            pltpu.VMEM((n_row - 1, sims, prows // n_row), jnp.float32),
            dma((chips,)), dma((chips,)), dma((chips - 1,)), dma((chips - 1,)), dma((n_row - 1,)), dma((n_row - 1,)),
        ],
        compiler_params=pltpu.CompilerParams(has_side_effects=True, vmem_limit_bytes=LIMIT),
        name="fold",
    )(acc)


def stream_kernel(n_col, units, p_ref, o_ref, *refs):
    priors, (apod_ref, proj_ref) = refs[:n_col], refs[n_col:n_col + 2]
    re_ref, acc_ref = refs[n_col + 2:n_col + 4]
    keep, swap, near, fars, far, ws, wr, ss, sr, fs, fr, gs, gr = refs[n_col + 4:]
    r, c = lax.axis_index("row"), lax.axis_index("col")
    chips = n_col // 2
    core, chip = lax.rem(c, 2), lax.div(c, 2)
    sims, size = wr.shape[2:]
    g = pl.program_id(0)

    def near_copy(u):
        k, q = lax.rem(u, swap.shape[0]), lax.rem(u, near.shape[0])
        return remote(swap.at[k], near.at[q], ss.at[k], sr.at[q], r, chip * 2 + 1 - core)

    def far_copies(u):
        k, q = lax.rem(u, fars.shape[0]), lax.rem(u, far.shape[0])
        return [remote(fars.at[k, s], far.at[q, s], fs.at[k, s], fr.at[q, s], r, lax.rem(chip + s + 1, chips) * 2 + core)
                for s in range(chips - 1)]

    def weighted_copies(u):
        k, q = lax.rem(u, ws.shape[0]), lax.rem(u, wr.shape[0])
        return [remote(ws.at[k, d], wr.at[q, d - 1], gs.at[k, d - 1], gr.at[q, d - 1], r, lax.rem(c + d, n_col))
                for d in range(1, n_col)]

    @pl.when(g == 0)
    def _():
        acc_ref[...] = jnp.zeros_like(acc_ref)

    @pl.when((g >= D2) & (g < units + D2))
    def _():
        u = g - D2
        near_copy(u).wait_recv()

        @pl.when(u >= fars.shape[0])
        def _():
            for cp in far_copies(u - fars.shape[0]):
                cp.wait_send()

        k, q, e = lax.rem(u, fars.shape[0]), lax.rem(u, near.shape[0]), lax.rem(u, keep.shape[0])
        copies = far_copies(u)
        for s in range(chips - 1):
            away = slice((s + 1) * sims, (s + 2) * sims)
            fars[k, s] = (keep[e, away] + near[q, away].astype(jnp.float32)).astype(jnp.bfloat16)
            copies[s].start()
        keep[e, :sims] = keep[e, :sims] + near[q, :sims].astype(jnp.float32)

    @pl.when((g >= D3) & (g < units + D3))
    def _():
        u = g - D3
        for cp in far_copies(u):
            cp.wait_recv()

        @pl.when(u >= ws.shape[0])
        def _():
            for cp in weighted_copies(u - ws.shape[0]):
                cp.wait_send()

        k, q, e = lax.rem(u, ws.shape[0]), lax.rem(u, far.shape[0]), lax.rem(u, keep.shape[0])
        for i in range(n_col):
            lanes = slice(i * size, (i + 1) * size)
            total = keep[e, :sims, lanes]
            for s in range(chips - 1):
                total = total + far[q, s, :, lanes].astype(jnp.float32)
            total = priors[i][...] + total
            re_ref[i] = total
            ws[k, lax.rem(i - c + n_col, n_col)] = (apod_ref[i:i + 1, :] * total).astype(jnp.bfloat16)
        for cp in weighted_copies(u):
            cp.start()

    @pl.when(g < units)
    def _():
        k, e = lax.rem(g, swap.shape[0]), lax.rem(g, keep.shape[0])

        @pl.when(g >= swap.shape[0])
        def _():
            near_copy(g - swap.shape[0]).wait_send()

        kept = n_col * sims // 2
        rows = o_ref[...].reshape(n_col * size, o_ref.shape[2])
        value = lax.dot_general(p_ref[...], rows, NT, preferred_element_type=jnp.float32)
        swap[k] = value[kept:].astype(jnp.bfloat16)
        near_copy(g).start()
        keep[e] = value[:kept]

    @pl.when(g >= D4)
    def _():
        u = g - D4
        for cp in weighted_copies(u):
            cp.wait_recv()
        k, q = lax.rem(u, ws.shape[0]), lax.rem(u, wr.shape[0])
        w = jnp.concatenate([ws[k, 0]] + [wr[q, d] for d in range(n_col - 1)], axis=0)
        prows = proj_ref.shape[0]
        tile = min(512, prows)
        for j in range(0, prows, tile):
            value = lax.dot_general(w, proj_ref[j:j + tile, :], NT, preferred_element_type=jnp.float32)
            for d in range(n_col):
                acc_ref[d, :, j:j + tile] += value[d * sims:(d + 1) * sims]

    @pl.when(g == units + D4 - 1)
    def _():
        for b in range(min(units, swap.shape[0])):
            near_copy(units - 1 - b).wait_send()
        for b in range(min(units, fars.shape[0])):
            for cp in far_copies(units - 1 - b):
                cp.wait_send()
        for b in range(min(units, ws.shape[0])):
            for cp in weighted_copies(units - 1 - b):
                cp.wait_send()


def stream(picked, obs, prior, apod, proj, n_col):
    depth, (sims, rows), prows = obs.shape[1], prior.shape, proj.shape[0]
    slab = rows // n_col
    units = slab // math.gcd(slab, UNIT)
    size = slab // units
    kept = n_col * sims // 2
    chips = n_col // 2

    def at(g, lag):
        return jnp.clip(g - lag, 0, units - 1)

    n_near, n_far, n_got = 2 * D2, 2 * D3 + 2 - 2 * D2, 2 * D4 + 2 - 2 * D3
    n_ws = D4 - D3 + 2
    wide = n_col * size
    dma, bf16 = pltpu.SemaphoreType.DMA, jnp.bfloat16
    prior_specs = [pl.BlockSpec((sims, size), functools.partial(lambda g, i: (0, i * units + at(g, D3)), i=i)) for i in range(n_col)]
    return pl.pallas_call(
        functools.partial(stream_kernel, n_col, units),
        grid=(units + D4,),
        in_specs=[
            pl.BlockSpec(picked.shape, lambda g: (0, 0)),
            pl.BlockSpec((n_col, size, depth), lambda g: (0, at(g, 0), 0)),
            *prior_specs,
            pl.BlockSpec((n_col, size), lambda g: (0, at(g, D3))),
            pl.BlockSpec((prows, size), lambda g: (0, at(g, D4))),
        ],
        out_specs=[
            pl.BlockSpec((n_col, sims, size), lambda g: (0, 0, at(g, D3))),
            pl.BlockSpec((n_col, sims, prows), lambda g: (0, 0, 0)),
        ],
        out_shape=[
            jax.ShapeDtypeStruct((n_col, sims, slab), jnp.float32),
            jax.ShapeDtypeStruct((n_col, sims, prows), jnp.float32),
        ],
        scratch_shapes=[
            pltpu.VMEM((D3 + 1, kept, wide), jnp.float32),
            pltpu.VMEM((2, kept, wide), bf16),
            pltpu.VMEM((n_near, kept, wide), bf16),
            pltpu.VMEM((2, chips - 1, sims, wide), bf16),
            pltpu.VMEM((n_far, chips - 1, sims, wide), bf16),
            pltpu.VMEM((n_ws, n_col, sims, size), bf16),
            pltpu.VMEM((n_got, n_col - 1, sims, size), bf16),
            dma((2,)), dma((n_near,)), dma((2, chips - 1)), dma((n_far, chips - 1)),
            dma((n_ws, n_col - 1)), dma((n_got, n_col - 1)),
        ],
        compiler_params=pltpu.CompilerParams(has_side_effects=True, vmem_limit_bytes=LIMIT, dimension_semantics=("arbitrary",)),
        name="stream",
    )(picked, obs.reshape(n_col, slab, depth), *[prior] * n_col, apod.reshape(n_col, slab), proj)


def on_device(n_row, n_col, obs_panel, skies, panel_index, prior_sum, apod, proj_panel):
    rows_blk, sims = skies.shape
    local_idx = panel_index - lax.axis_index("row") * rows_blk
    inside = (local_idx >= 0) & (local_idx < rows_blk)
    taken = jnp.take(skies, jnp.clip(local_idx, 0, rows_blk - 1), axis=0)
    own = jnp.where(inside[:, None], taken, jnp.zeros((), jnp.bfloat16)).T
    picked = spread(own, n_row, n_col)

    out, acc = stream(picked, obs_panel, prior_sum.T, apod, proj_panel, n_col)
    projection = fold(acc, n_row, n_col)
    return out.transpose(0, 2, 1).reshape(rows_blk, sims), projection.T


def solution(mesh):
    in_specs = (P("row", "col"), P("row", "col"), P(), P("row", "col"), P("row"), P(None, ("row", "col")))
    out_specs = (P("row", "col"), P("row", "col"))
    body = functools.partial(on_device, mesh.shape["row"], mesh.shape["col"])
    return jax.shard_map(body, mesh=mesh, in_specs=in_specs, out_specs=out_specs, check_vma=False)
```

```python
import functools
import math

import jax
import jax.numpy as jnp
from jax import lax
from jax.experimental import pallas as pl
from jax.experimental.pallas import tpu as pltpu
from jax.sharding import PartitionSpec as P

MESH = pl.DeviceIdType.MESH
NT = (((1,), (1,)), ((), ()))
UNIT = 256
D2, D3, D4 = 1, 3, 5
LIMIT = 48 * 1024 * 1024


def remote(src, dst, send, recv, row, col):
    return pltpu.make_async_remote_copy(
        src_ref=src, dst_ref=dst, send_sem=send, recv_sem=recv, device_id=(row, col), device_id_type=MESH
    )


def spread_kernel(n_row, n_col, own_ref, out_ref, land, mine, gather, send1, recv1, send2, recv2):
    r, c = lax.axis_index("row"), lax.axis_index("col")
    sims, panel = own_ref.shape
    part = panel // n_row
    rep = n_row // n_col

    def part_of(row):
        return lax.rem(row, 2) * (n_row // 2) + lax.div(row, 2)

    first = []
    for d in range(1, n_row):
        to = lax.rem(r + d, n_row)
        cp = remote(own_ref.at[:, pl.ds(pl.multiple_of(part_of(to) * part, part), part)], land.at[d - 1],
                    send1.at[d - 1], recv1.at[d - 1], to, c)
        cp.start()
        first.append(cp)
    total = own_ref[:, pl.ds(pl.multiple_of(part_of(r) * part, part), part)].astype(jnp.float32)
    for d in range(1, n_row):
        first[d - 1].wait_recv()
        total = total + land[d - 1].astype(jnp.float32)
    mine[...] = total.astype(mine.dtype)
    sub = lax.rem(part_of(r), rep)
    col_to = lax.div(part_of(r), rep)
    slot = sub * n_col + c
    second = []
    for d in range(n_row):
        to = lax.rem(r + d, n_row)
        cp = remote(mine, gather.at[slot], send2.at[d], recv2.at[slot], to, col_to)
        second.append(cp)
        if d > 0:
            cp.start()
        else:
            @pl.when(col_to != c)
            def _():
                cp.start()

            @pl.when(col_to == c)
            def _():
                gather[slot] = mine[...]
    for s in range(rep):
        for j in range(n_col):
            here = (c * rep + s == part_of(r)) & (c == j)

            @pl.when(jnp.logical_not(here))
            def _():
                remote(mine, gather.at[s * n_col + j], send2.at[0], recv2.at[s * n_col + j], r, c).wait_recv()
    chips = n_col // 2
    core, chip = lax.rem(c, 2), lax.div(c, 2)
    for q in range(n_col):
        other, shift = q // chips, q % chips
        source = lax.rem(chip + shift, chips) * 2 + (core if other == 0 else 1 - core)
        for s in range(rep):
            out_ref[q * sims:(q + 1) * sims, s * part:(s + 1) * part] = gather[s * n_col + source]
    for cp in first:
        cp.wait_send()
    for d in range(n_row):
        if d > 0:
            second[d].wait_send()
        else:
            @pl.when(col_to != c)
            def _():
                second[0].wait_send()


def spread(own, n_row, n_col):
    sims, panel = own.shape
    part = panel // n_row
    vmem = pl.BlockSpec(memory_space=pltpu.VMEM)
    return pl.pallas_call(
        functools.partial(spread_kernel, n_row, n_col),
        out_shape=jax.ShapeDtypeStruct((sims * n_col, panel // n_col), own.dtype),
        in_specs=[vmem],
        out_specs=vmem,
        scratch_shapes=[
            pltpu.VMEM((n_row - 1, sims, part), own.dtype),
            pltpu.VMEM((sims, part), own.dtype),
            pltpu.VMEM((n_row, sims, part), own.dtype),
            pltpu.SemaphoreType.DMA((n_row - 1,)),
            pltpu.SemaphoreType.DMA((n_row - 1,)),
            pltpu.SemaphoreType.DMA((n_row,)),
            pltpu.SemaphoreType.DMA((n_row,)),
        ],
        compiler_params=pltpu.CompilerParams(has_side_effects=True, vmem_limit_bytes=LIMIT),
        name="spread",
    )(own)


def fold_kernel(n_row, n_col, acc_ref, swapped_ref, out_ref, sa, lx0, b0, ly0, ly1, b1, lx1, ends, lz,
                sx0, rx0, sy, ry, sx1, rx1, sz, rz):
    r, c = lax.axis_index("row"), lax.axis_index("col")
    chips, pairs = n_col // 2, n_row // 2
    core, chip = lax.rem(c, 2), lax.div(c, 2)
    low, high = lax.rem(r, 2), lax.div(r, 2)
    beside = high * 2 + 1 - low
    sims, pb = out_ref.shape
    hs, half = sims // 2, pairs * pb

    def side(which):
        return pl.ds(pl.multiple_of(which * half, half), half)

    def to_col(s):
        return lax.rem(chip + s, chips) * 2 + core

    copies = []

    def go(*args):
        cp = remote(*args)
        cp.start()
        copies.append(cp)
        return cp

    order = list(range(1, chips)) + [0]
    x0 = []
    for s in order:
        mine = (chips - s) % chips
        theirs = lax.rem(2 * chips - s - core, chips)
        for k in range(n_row):
            from_lanes = slice(k * pb, (k + 1) * pb)
            at = (k % 2) * half + (k // 2) * pb
            for h in range(2):
                rows = slice(h * hs, (h + 1) * hs)
                sa[h, s, :, at:at + pb] = acc_ref[mine, rows, from_lanes] + swapped_ref[theirs, rows, from_lanes]
        if s > 0:
            x0.append(go(sa.at[0, s], lx0.at[s - 1], sx0.at[s - 1], rx0.at[s - 1], r, to_col(s)))
    y1 = go(sa.at[1, :, :, side(1 - low)], ly1, sy.at[1], ry.at[1], beside, c)
    total = sa[0, 0]
    for s in range(1, chips):
        x0[s - 1].wait_recv()
        total = total + lx0[s - 1]
    b0[...] = total
    y0 = go(b0.at[:, side(1 - low)], ly0, sy.at[0], ry.at[0], beside, c)
    y1.wait_recv()
    b1[...] = sa[1, :, :, side(low)] + ly1[...]
    x1 = [go(b1.at[s], lx1.at[s - 1], sx1.at[s - 1], rx1.at[s - 1], r, to_col(s)) for s in range(1, chips)]
    z = []
    for h in range(2):
        if h == 0:
            y0.wait_recv()
            ends[0] = b0[:, side(low)] + ly0[...]
        else:
            total = b1[0]
            for s in range(1, chips):
                x1[s - 1].wait_recv()
                total = total + lx1[s - 1]
            ends[1] = total
        for d in range(1, pairs):
            to = lax.rem(high + d, pairs)
            z.append(go(ends.at[h, :, pl.ds(pl.multiple_of(to * pb, pb), pb)], lz.at[h, d - 1], sz.at[h, d - 1], rz.at[h, d - 1], to * 2 + low, c))
    for h in range(2):
        total = ends[h, :, pl.ds(pl.multiple_of(high * pb, pb), pb)]
        for d in range(1, pairs):
            z[h * (pairs - 1) + d - 1].wait_recv()
            total = total + lz[h, d - 1]
        out_ref[h * hs:(h + 1) * hs, :] = total
    for cp in copies:
        cp.wait_send()


def fold(acc, swapped, n_row, n_col):
    _, sims, prows = acc.shape
    chips, pairs = n_col // 2, n_row // 2
    hs, pb, half = sims // 2, prows // n_row, prows // 2
    vmem = pl.BlockSpec(memory_space=pltpu.VMEM)
    dma = pltpu.SemaphoreType.DMA

    def f32(*shape):
        return pltpu.VMEM(shape, jnp.float32)

    return pl.pallas_call(
        functools.partial(fold_kernel, n_row, n_col),
        out_shape=jax.ShapeDtypeStruct((sims, pb), jnp.float32),
        in_specs=[vmem] * 2,
        out_specs=vmem,
        scratch_shapes=[
            f32(2, chips, hs, prows), f32(chips - 1, hs, prows), f32(hs, prows), f32(hs, half),
            f32(chips, hs, half), f32(chips, hs, half), f32(chips - 1, hs, half), f32(2, hs, half), f32(2, pairs - 1, hs, pb),
            dma((chips - 1,)), dma((chips - 1,)), dma((2,)), dma((2,)),
            dma((chips - 1,)), dma((chips - 1,)), dma((2, pairs - 1)), dma((2, pairs - 1)),
        ],
        compiler_params=pltpu.CompilerParams(has_side_effects=True, vmem_limit_bytes=LIMIT),
        name="fold",
    )(acc, swapped)


def stream_kernel(n_col, units, p_ref, o_ref, *refs):
    priors, (apod_ref, proj_ref) = refs[:n_col], refs[n_col:n_col + 2]
    re_ref, *accs = refs[n_col + 2:n_col + 5]
    keep, swap, near, fars, far, ws, wr, ss, sr, fs, fr, gs, gr = refs[n_col + 5:]
    r, c = lax.axis_index("row"), lax.axis_index("col")
    chips = n_col // 2
    core, chip = lax.rem(c, 2), lax.div(c, 2)
    sims, size = wr.shape[2:]
    g = pl.program_id(0)

    def near_copy(u):
        k, q = lax.rem(u, swap.shape[0]), lax.rem(u, near.shape[0])
        return remote(swap.at[k], near.at[q], ss.at[k], sr.at[q], r, chip * 2 + 1 - core)

    def far_copies(u):
        k, q = lax.rem(u, fars.shape[0]), lax.rem(u, far.shape[0])
        return [remote(fars.at[k, s], far.at[q, s], fs.at[k, s], fr.at[q, s], r, lax.rem(chip + s + 1, chips) * 2 + core)
                for s in range(chips - 1)]

    def weighted_copies(u):
        k, q = lax.rem(u, ws.shape[0]), lax.rem(u, wr.shape[0])
        return [remote(ws.at[k, d], wr.at[q, d - 1], gs.at[k, d - 1], gr.at[q, d - 1], r, lax.rem(c + d, n_col))
                for d in range(1, n_col)]

    @pl.when(g == 0)
    def _():
        for acc in accs:
            acc[...] = jnp.zeros_like(acc)

    @pl.when((g >= D2) & (g < units + D2))
    def _():
        u = g - D2
        near_copy(u).wait_recv()

        @pl.when(u >= fars.shape[0])
        def _():
            for cp in far_copies(u - fars.shape[0]):
                cp.wait_send()

        k, q, e = lax.rem(u, fars.shape[0]), lax.rem(u, near.shape[0]), lax.rem(u, keep.shape[0])
        copies = far_copies(u)
        for s in range(chips - 1):
            away = slice((s + 1) * sims, (s + 2) * sims)
            fars[k, s] = (keep[e, away] + near[q, away].astype(jnp.float32)).astype(jnp.bfloat16)
            copies[s].start()
        keep[e, :sims] = keep[e, :sims] + near[q, :sims].astype(jnp.float32)

    @pl.when((g >= D3) & (g < units + D3))
    def _():
        u = g - D3
        for cp in far_copies(u):
            cp.wait_recv()

        @pl.when(u >= ws.shape[0])
        def _():
            for cp in weighted_copies(u - ws.shape[0]):
                cp.wait_send()

        k, q, e = lax.rem(u, ws.shape[0]), lax.rem(u, far.shape[0]), lax.rem(u, keep.shape[0])
        for i in range(n_col):
            lanes = slice(i * size, (i + 1) * size)
            total = keep[e, :sims, lanes]
            for s in range(chips - 1):
                total = total + far[q, s, :, lanes].astype(jnp.float32)
            total = priors[i][...] + total
            re_ref[i] = total
            ws[k, lax.rem(i - c + n_col, n_col)] = (apod_ref[i:i + 1, :] * total).astype(jnp.bfloat16)
        for cp in weighted_copies(u):
            cp.start()

    @pl.when(g < units)
    def _():
        k, e = lax.rem(g, swap.shape[0]), lax.rem(g, keep.shape[0])

        @pl.when(g >= swap.shape[0])
        def _():
            near_copy(g - swap.shape[0]).wait_send()

        kept = n_col * sims // 2
        rows = o_ref[...].reshape(n_col * size, o_ref.shape[2])
        value = lax.dot_general(p_ref[...], rows, NT, preferred_element_type=jnp.float32)
        swap[k] = value[kept:].astype(jnp.bfloat16)
        near_copy(g).start()
        keep[e] = value[:kept]

    @pl.when(g >= D4)
    def _():
        u = g - D4
        for cp in weighted_copies(u):
            cp.wait_recv()
        k, q = lax.rem(u, ws.shape[0]), lax.rem(u, wr.shape[0])
        w = jnp.concatenate([ws[k, 0]] + [wr[q, d] for d in range(n_col - 1)], axis=0)
        prows = proj_ref.shape[0]
        tile = min(512, prows)
        for j in range(0, prows, tile):
            value = lax.dot_general(w, proj_ref[j:j + tile, :], NT, preferred_element_type=jnp.float32)
            for d in range(n_col):
                accs[d % 2][d // 2, :, j:j + tile] += value[d * sims:(d + 1) * sims]

    @pl.when(g == units + D4 - 1)
    def _():
        for b in range(min(units, swap.shape[0])):
            near_copy(units - 1 - b).wait_send()
        for b in range(min(units, fars.shape[0])):
            for cp in far_copies(units - 1 - b):
                cp.wait_send()
        for b in range(min(units, ws.shape[0])):
            for cp in weighted_copies(units - 1 - b):
                cp.wait_send()


def stream(picked, obs, prior, apod, proj, n_col):
    depth, (sims, rows), prows = obs.shape[1], prior.shape, proj.shape[0]
    slab = rows // n_col
    units = slab // math.gcd(slab, UNIT)
    size = slab // units
    kept = n_col * sims // 2
    chips = n_col // 2

    def at(g, lag):
        return jnp.clip(g - lag, 0, units - 1)

    n_near, n_far, n_got = 2 * D2, 2 * D3 + 2 - 2 * D2, 2 * D4 + 2 - 2 * D3
    n_ws = D4 - D3 + 2
    wide = n_col * size
    dma, bf16 = pltpu.SemaphoreType.DMA, jnp.bfloat16
    prior_specs = [pl.BlockSpec((sims, size), functools.partial(lambda g, i: (0, i * units + at(g, D3)), i=i)) for i in range(n_col)]
    return pl.pallas_call(
        functools.partial(stream_kernel, n_col, units),
        grid=(units + D4,),
        in_specs=[
            pl.BlockSpec(picked.shape, lambda g: (0, 0)),
            pl.BlockSpec((n_col, size, depth), lambda g: (0, at(g, 0), 0)),
            *prior_specs,
            pl.BlockSpec((n_col, size), lambda g: (0, at(g, D3))),
            pl.BlockSpec((prows, size), lambda g: (0, at(g, D4))),
        ],
        out_specs=[
            pl.BlockSpec((n_col, sims, size), lambda g: (0, 0, at(g, D3))),
            *[pl.BlockSpec((chips, sims, prows), lambda g: (0, 0, 0))] * 2,
        ],
        out_shape=[
            jax.ShapeDtypeStruct((n_col, sims, slab), jnp.float32),
            *[jax.ShapeDtypeStruct((chips, sims, prows), jnp.float32)] * 2,
        ],
        scratch_shapes=[
            pltpu.VMEM((D3 + 1, kept, wide), jnp.float32),
            pltpu.VMEM((2, kept, wide), bf16),
            pltpu.VMEM((n_near, kept, wide), bf16),
            pltpu.VMEM((2, chips - 1, sims, wide), bf16),
            pltpu.VMEM((n_far, chips - 1, sims, wide), bf16),
            pltpu.VMEM((n_ws, n_col, sims, size), bf16),
            pltpu.VMEM((n_got, n_col - 1, sims, size), bf16),
            dma((2,)), dma((n_near,)), dma((2, chips - 1)), dma((n_far, chips - 1)),
            dma((n_ws, n_col - 1)), dma((n_got, n_col - 1)),
        ],
        compiler_params=pltpu.CompilerParams(has_side_effects=True, vmem_limit_bytes=LIMIT, dimension_semantics=("arbitrary",)),
        name="stream",
    )(picked, obs.reshape(n_col, slab, depth), *[prior] * n_col, apod.reshape(n_col, slab), proj)


def on_device(n_row, n_col, obs_panel, skies, panel_index, prior_sum, apod, proj_panel):
    rows_blk, sims = skies.shape
    local_idx = panel_index - lax.axis_index("row") * rows_blk
    inside = (local_idx >= 0) & (local_idx < rows_blk)
    taken = jnp.take(skies, jnp.clip(local_idx, 0, rows_blk - 1), axis=0)
    own = jnp.where(inside[:, None], taken, jnp.zeros((), jnp.bfloat16)).T
    picked = spread(own, n_row, n_col)

    out, acc, other = stream(picked, obs_panel, prior_sum.T, apod, proj_panel, n_col)
    swapped = lax.ppermute(other, "col", [(i, i ^ 1) for i in range(n_col)])
    projection = fold(acc, swapped, n_row, n_col)
    return out.transpose(0, 2, 1).reshape(rows_blk, sims), projection.T


def solution(mesh):
    in_specs = (P("row", "col"), P("row", "col"), P(), P("row", "col"), P("row"), P(None, ("row", "col")))
    out_specs = (P("row", "col"), P("row", "col"))
    body = functools.partial(on_device, mesh.shape["row"], mesh.shape["col"])
    return jax.shard_map(body, mesh=mesh, in_specs=in_specs, out_specs=out_specs, check_vma=False)
```

```python
import functools
import math

import jax
import jax.numpy as jnp
from jax import lax
from jax.experimental import pallas as pl
from jax.experimental.pallas import tpu as pltpu
from jax.sharding import PartitionSpec as P

MESH = pl.DeviceIdType.MESH
NT = (((1,), (1,)), ((), ()))
UNIT = 256
D2, D3, D4 = 1, 3, 5
LIMIT = 48 * 1024 * 1024


def remote(src, dst, send, recv, row, col):
    return pltpu.make_async_remote_copy(
        src_ref=src, dst_ref=dst, send_sem=send, recv_sem=recv, device_id=(row, col), device_id_type=MESH
    )


def meet(devices):
    barrier = pltpu.get_barrier_semaphore()
    for device in devices:
        pl.semaphore_signal(barrier, inc=1, device_id=device, device_id_type=MESH)
    pl.semaphore_wait(barrier, len(devices))


def meet_all(n_row, n_col):
    barrier = pltpu.get_barrier_semaphore()
    me = lax.axis_index("row") * n_col + lax.axis_index("col")
    every = n_row * n_col

    def tell(i, carry):
        to = lax.rem(me + i, every)
        pl.semaphore_signal(barrier, inc=1, device_id=(lax.div(to, n_col), lax.rem(to, n_col)), device_id_type=MESH)
        return carry

    lax.fori_loop(1, every, tell, 0)
    pl.semaphore_wait(barrier, every - 1)


def spread_kernel(n_row, n_col, own_ref, out_ref, land, mine, gather, send1, recv1, send2, recv2):
    r, c = lax.axis_index("row"), lax.axis_index("col")
    meet_all(n_row, n_col)
    sims, panel = own_ref.shape
    part = panel // n_row
    rep = n_row // n_col

    def part_of(row):
        return lax.rem(row, 2) * (n_row // 2) + lax.div(row, 2)

    first = []
    for d in range(1, n_row):
        to = lax.rem(r + d, n_row)
        cp = remote(own_ref.at[:, pl.ds(pl.multiple_of(part_of(to) * part, part), part)], land.at[d - 1],
                    send1.at[d - 1], recv1.at[d - 1], to, c)
        cp.start()
        first.append(cp)
    total = own_ref[:, pl.ds(pl.multiple_of(part_of(r) * part, part), part)].astype(jnp.float32)
    for d in range(1, n_row):
        first[d - 1].wait_recv()
        total = total + land[d - 1].astype(jnp.float32)
    mine[...] = total.astype(mine.dtype)
    sub = lax.rem(part_of(r), rep)
    col_to = lax.div(part_of(r), rep)
    slot = sub * n_col + c
    second = []
    for d in range(n_row):
        to = lax.rem(r + d, n_row)
        cp = remote(mine, gather.at[slot], send2.at[d], recv2.at[slot], to, col_to)
        second.append(cp)
        if d > 0:
            cp.start()
        else:
            @pl.when(col_to != c)
            def _():
                cp.start()

            @pl.when(col_to == c)
            def _():
                gather[slot] = mine[...]
    for s in range(rep):
        for j in range(n_col):
            here = (c * rep + s == part_of(r)) & (c == j)

            @pl.when(jnp.logical_not(here))
            def _():
                remote(mine, gather.at[s * n_col + j], send2.at[0], recv2.at[s * n_col + j], r, c).wait_recv()
    chips = n_col // 2
    core, chip = lax.rem(c, 2), lax.div(c, 2)
    for q in range(n_col):
        other, shift = q // chips, q % chips
        source = lax.rem(chip + shift, chips) * 2 + (core if other == 0 else 1 - core)
        for s in range(rep):
            out_ref[q * sims:(q + 1) * sims, s * part:(s + 1) * part] = gather[s * n_col + source]
    for cp in first:
        cp.wait_send()
    for d in range(n_row):
        if d > 0:
            second[d].wait_send()
        else:
            @pl.when(col_to != c)
            def _():
                second[0].wait_send()


def spread(own, n_row, n_col):
    sims, panel = own.shape
    part = panel // n_row
    vmem = pl.BlockSpec(memory_space=pltpu.VMEM)
    return pl.pallas_call(
        functools.partial(spread_kernel, n_row, n_col),
        out_shape=jax.ShapeDtypeStruct((sims * n_col, panel // n_col), own.dtype),
        in_specs=[vmem],
        out_specs=vmem,
        scratch_shapes=[
            pltpu.VMEM((n_row - 1, sims, part), own.dtype),
            pltpu.VMEM((sims, part), own.dtype),
            pltpu.VMEM((n_row, sims, part), own.dtype),
            pltpu.SemaphoreType.DMA((n_row - 1,)),
            pltpu.SemaphoreType.DMA((n_row - 1,)),
            pltpu.SemaphoreType.DMA((n_row,)),
            pltpu.SemaphoreType.DMA((n_row,)),
        ],
        compiler_params=pltpu.CompilerParams(has_side_effects=True, collective_id=0, vmem_limit_bytes=LIMIT),
        name="spread",
    )(own)


def fold_kernel(n_row, n_col, acc_ref, swapped_ref, out_ref, sa, lx0, b0, ly0, ly1, b1, lx1, ends, lz,
                sx0, rx0, sy, ry, sx1, rx1, sz, rz):
    r, c = lax.axis_index("row"), lax.axis_index("col")
    chips, pairs = n_col // 2, n_row // 2
    core, chip = lax.rem(c, 2), lax.div(c, 2)
    low, high = lax.rem(r, 2), lax.div(r, 2)
    beside = high * 2 + 1 - low
    meet([(r, lax.rem(chip + s, chips) * 2 + core) for s in range(1, chips)]
         + [(beside, c)] + [(lax.rem(high + d, pairs) * 2 + low, c) for d in range(1, pairs)])
    sims, pb = out_ref.shape
    hs, half = sims // 2, pairs * pb

    def side(which):
        return pl.ds(pl.multiple_of(which * half, half), half)

    def to_col(s):
        return lax.rem(chip + s, chips) * 2 + core

    copies = []

    def go(*args):
        cp = remote(*args)
        cp.start()
        copies.append(cp)
        return cp

    order = list(range(1, chips)) + [0]
    x0 = []
    for s in order:
        mine = (chips - s) % chips
        theirs = lax.rem(2 * chips - s - core, chips)
        for k in range(n_row):
            from_lanes = slice(k * pb, (k + 1) * pb)
            at = (k % 2) * half + (k // 2) * pb
            for h in range(2):
                rows = slice(h * hs, (h + 1) * hs)
                sa[h, s, :, at:at + pb] = acc_ref[mine, rows, from_lanes] + swapped_ref[theirs, rows, from_lanes]
        if s > 0:
            x0.append(go(sa.at[0, s], lx0.at[s - 1], sx0.at[s - 1], rx0.at[s - 1], r, to_col(s)))
    y1 = go(sa.at[1, :, :, side(1 - low)], ly1, sy.at[1], ry.at[1], beside, c)
    total = sa[0, 0]
    for s in range(1, chips):
        x0[s - 1].wait_recv()
        total = total + lx0[s - 1]
    b0[...] = total
    y0 = go(b0.at[:, side(1 - low)], ly0, sy.at[0], ry.at[0], beside, c)
    y1.wait_recv()
    b1[...] = sa[1, :, :, side(low)] + ly1[...]
    x1 = [go(b1.at[s], lx1.at[s - 1], sx1.at[s - 1], rx1.at[s - 1], r, to_col(s)) for s in range(1, chips)]
    z = []
    for h in range(2):
        if h == 0:
            y0.wait_recv()
            ends[0] = b0[:, side(low)] + ly0[...]
        else:
            total = b1[0]
            for s in range(1, chips):
                x1[s - 1].wait_recv()
                total = total + lx1[s - 1]
            ends[1] = total
        for d in range(1, pairs):
            to = lax.rem(high + d, pairs)
            z.append(go(ends.at[h, :, pl.ds(pl.multiple_of(to * pb, pb), pb)], lz.at[h, d - 1], sz.at[h, d - 1], rz.at[h, d - 1], to * 2 + low, c))
    for h in range(2):
        total = ends[h, :, pl.ds(pl.multiple_of(high * pb, pb), pb)]
        for d in range(1, pairs):
            z[h * (pairs - 1) + d - 1].wait_recv()
            total = total + lz[h, d - 1]
        out_ref[h * hs:(h + 1) * hs, :] = total
    for cp in copies:
        cp.wait_send()


def fold(acc, swapped, n_row, n_col):
    _, sims, prows = acc.shape
    chips, pairs = n_col // 2, n_row // 2
    hs, pb, half = sims // 2, prows // n_row, prows // 2
    vmem = pl.BlockSpec(memory_space=pltpu.VMEM)
    dma = pltpu.SemaphoreType.DMA

    def f32(*shape):
        return pltpu.VMEM(shape, jnp.float32)

    return pl.pallas_call(
        functools.partial(fold_kernel, n_row, n_col),
        out_shape=jax.ShapeDtypeStruct((sims, pb), jnp.float32),
        in_specs=[vmem] * 2,
        out_specs=vmem,
        scratch_shapes=[
            f32(2, chips, hs, prows), f32(chips - 1, hs, prows), f32(hs, prows), f32(hs, half),
            f32(chips, hs, half), f32(chips, hs, half), f32(chips - 1, hs, half), f32(2, hs, half), f32(2, pairs - 1, hs, pb),
            dma((chips - 1,)), dma((chips - 1,)), dma((2,)), dma((2,)),
            dma((chips - 1,)), dma((chips - 1,)), dma((2, pairs - 1)), dma((2, pairs - 1)),
        ],
        compiler_params=pltpu.CompilerParams(has_side_effects=True, collective_id=1, vmem_limit_bytes=LIMIT),
        name="fold",
    )(acc, swapped)


def stream_kernel(n_col, units, p_ref, o_ref, *refs):
    priors, (apod_ref, proj_ref) = refs[:n_col], refs[n_col:n_col + 2]
    re_ref, *accs = refs[n_col + 2:n_col + 5]
    keep, swap, near, fars, far, ws, wr, ss, sr, fs, fr, gs, gr = refs[n_col + 5:]
    r, c = lax.axis_index("row"), lax.axis_index("col")
    chips = n_col // 2
    core, chip = lax.rem(c, 2), lax.div(c, 2)
    sims, size = wr.shape[2:]
    g = pl.program_id(0)

    def near_copy(u):
        k, q = lax.rem(u, swap.shape[0]), lax.rem(u, near.shape[0])
        return remote(swap.at[k], near.at[q], ss.at[k], sr.at[q], r, chip * 2 + 1 - core)

    def far_copies(u):
        k, q = lax.rem(u, fars.shape[0]), lax.rem(u, far.shape[0])
        return [remote(fars.at[k, s], far.at[q, s], fs.at[k, s], fr.at[q, s], r, lax.rem(chip + s + 1, chips) * 2 + core)
                for s in range(chips - 1)]

    def weighted_copies(u):
        k, q = lax.rem(u, ws.shape[0]), lax.rem(u, wr.shape[0])
        return [remote(ws.at[k, d], wr.at[q, d - 1], gs.at[k, d - 1], gr.at[q, d - 1], r, lax.rem(c + d, n_col))
                for d in range(1, n_col)]

    @pl.when(g == 0)
    def _():
        meet([(r, lax.rem(c + d, n_col)) for d in range(1, n_col)])
        for acc in accs:
            acc[...] = jnp.zeros_like(acc)

    @pl.when((g >= D2) & (g < units + D2))
    def _():
        u = g - D2
        near_copy(u).wait_recv()

        @pl.when(u >= fars.shape[0])
        def _():
            for cp in far_copies(u - fars.shape[0]):
                cp.wait_send()

        k, q, e = lax.rem(u, fars.shape[0]), lax.rem(u, near.shape[0]), lax.rem(u, keep.shape[0])
        copies = far_copies(u)
        for s in range(chips - 1):
            away = slice((s + 1) * sims, (s + 2) * sims)
            fars[k, s] = (keep[e, away] + near[q, away].astype(jnp.float32)).astype(jnp.bfloat16)
            copies[s].start()
        keep[e, :sims] = keep[e, :sims] + near[q, :sims].astype(jnp.float32)

    @pl.when((g >= D3) & (g < units + D3))
    def _():
        u = g - D3
        for cp in far_copies(u):
            cp.wait_recv()

        @pl.when(u >= ws.shape[0])
        def _():
            for cp in weighted_copies(u - ws.shape[0]):
                cp.wait_send()

        k, q, e = lax.rem(u, ws.shape[0]), lax.rem(u, far.shape[0]), lax.rem(u, keep.shape[0])
        for i in range(n_col):
            lanes = slice(i * size, (i + 1) * size)
            total = keep[e, :sims, lanes]
            for s in range(chips - 1):
                total = total + far[q, s, :, lanes].astype(jnp.float32)
            total = priors[i][...] + total
            re_ref[i] = total
            ws[k, lax.rem(i - c + n_col, n_col)] = (apod_ref[i:i + 1, :] * total).astype(jnp.bfloat16)
        for cp in weighted_copies(u):
            cp.start()

    @pl.when(g < units)
    def _():
        k, e = lax.rem(g, swap.shape[0]), lax.rem(g, keep.shape[0])

        @pl.when(g >= swap.shape[0])
        def _():
            near_copy(g - swap.shape[0]).wait_send()

        kept = n_col * sims // 2
        rows = o_ref[...].reshape(n_col * size, o_ref.shape[2])
        value = lax.dot_general(p_ref[...], rows, NT, preferred_element_type=jnp.float32)
        swap[k] = value[kept:].astype(jnp.bfloat16)
        near_copy(g).start()
        keep[e] = value[:kept]

    @pl.when(g >= D4)
    def _():
        u = g - D4
        for cp in weighted_copies(u):
            cp.wait_recv()
        k, q = lax.rem(u, ws.shape[0]), lax.rem(u, wr.shape[0])
        w = jnp.concatenate([ws[k, 0]] + [wr[q, d] for d in range(n_col - 1)], axis=0)
        prows = proj_ref.shape[0]
        tile = min(512, prows)
        for j in range(0, prows, tile):
            value = lax.dot_general(w, proj_ref[j:j + tile, :], NT, preferred_element_type=jnp.float32)
            for d in range(n_col):
                accs[d % 2][d // 2, :, j:j + tile] += value[d * sims:(d + 1) * sims]

    @pl.when(g == units + D4 - 1)
    def _():
        for b in range(min(units, swap.shape[0])):
            near_copy(units - 1 - b).wait_send()
        for b in range(min(units, fars.shape[0])):
            for cp in far_copies(units - 1 - b):
                cp.wait_send()
        for b in range(min(units, ws.shape[0])):
            for cp in weighted_copies(units - 1 - b):
                cp.wait_send()


def stream(picked, obs, prior, apod, proj, n_col):
    depth, (sims, rows), prows = obs.shape[1], prior.shape, proj.shape[0]
    slab = rows // n_col
    units = slab // math.gcd(slab, UNIT)
    size = slab // units
    kept = n_col * sims // 2
    chips = n_col // 2

    def at(g, lag):
        return jnp.clip(g - lag, 0, units - 1)

    n_near, n_far, n_got = 2 * D2, 2 * D3 + 2 - 2 * D2, 2 * D4 + 2 - 2 * D3
    n_ws = D4 - D3 + 2
    wide = n_col * size
    dma, bf16 = pltpu.SemaphoreType.DMA, jnp.bfloat16
    prior_specs = [pl.BlockSpec((sims, size), functools.partial(lambda g, i: (0, i * units + at(g, D3)), i=i)) for i in range(n_col)]
    return pl.pallas_call(
        functools.partial(stream_kernel, n_col, units),
        grid=(units + D4,),
        in_specs=[
            pl.BlockSpec(picked.shape, lambda g: (0, 0)),
            pl.BlockSpec((n_col, size, depth), lambda g: (0, at(g, 0), 0)),
            *prior_specs,
            pl.BlockSpec((n_col, size), lambda g: (0, at(g, D3))),
            pl.BlockSpec((prows, size), lambda g: (0, at(g, D4))),
        ],
        out_specs=[
            pl.BlockSpec((n_col, sims, size), lambda g: (0, 0, at(g, D3))),
            *[pl.BlockSpec((chips, sims, prows), lambda g: (0, 0, 0))] * 2,
        ],
        out_shape=[
            jax.ShapeDtypeStruct((n_col, sims, slab), jnp.float32),
            *[jax.ShapeDtypeStruct((chips, sims, prows), jnp.float32)] * 2,
        ],
        scratch_shapes=[
            pltpu.VMEM((D3 + 1, kept, wide), jnp.float32),
            pltpu.VMEM((2, kept, wide), bf16),
            pltpu.VMEM((n_near, kept, wide), bf16),
            pltpu.VMEM((2, chips - 1, sims, wide), bf16),
            pltpu.VMEM((n_far, chips - 1, sims, wide), bf16),
            pltpu.VMEM((n_ws, n_col, sims, size), bf16),
            pltpu.VMEM((n_got, n_col - 1, sims, size), bf16),
            dma((2,)), dma((n_near,)), dma((2, chips - 1)), dma((n_far, chips - 1)),
            dma((n_ws, n_col - 1)), dma((n_got, n_col - 1)),
        ],
        compiler_params=pltpu.CompilerParams(has_side_effects=True, collective_id=2, vmem_limit_bytes=LIMIT, dimension_semantics=("arbitrary",)),
        name="stream",
    )(picked, obs.reshape(n_col, slab, depth), *[prior] * n_col, apod.reshape(n_col, slab), proj)


def on_device(n_row, n_col, obs_panel, skies, panel_index, prior_sum, apod, proj_panel):
    rows_blk, sims = skies.shape
    local_idx = panel_index - lax.axis_index("row") * rows_blk
    inside = (local_idx >= 0) & (local_idx < rows_blk)
    taken = jnp.take(skies, jnp.clip(local_idx, 0, rows_blk - 1), axis=0)
    own = jnp.where(inside[:, None], taken, jnp.zeros((), jnp.bfloat16)).T
    picked = spread(own, n_row, n_col)

    out, acc, other = stream(picked, obs_panel, prior_sum.T, apod, proj_panel, n_col)
    swapped = lax.ppermute(other, "col", [(i, i ^ 1) for i in range(n_col)])
    projection = fold(acc, swapped, n_row, n_col)
    return out.transpose(0, 2, 1).reshape(rows_blk, sims), projection.T


def solution(mesh):
    in_specs = (P("row", "col"), P("row", "col"), P(), P("row", "col"), P("row"), P(None, ("row", "col")))
    out_specs = (P("row", "col"), P("row", "col"))
    body = functools.partial(on_device, mesh.shape["row"], mesh.shape["col"])
    return jax.shard_map(body, mesh=mesh, in_specs=in_specs, out_specs=out_specs, check_vma=False)
```
